32 devices in a mesh: head: 4 (over y, x), seq: 8 (over z, core).
Axes of the slice: x: 2, y: 2, z: 4, core: 2. Of those that a mesh axis runs over, the one named last changes fastest.
Arguments:
- queries: bfloat16 [4096, 8192], P('seq', 'head'), may hold values from -200 to 200
- keys: bfloat16 [4096, 8192], P('seq', 'head'), may hold values from -6 to 6
- values: bfloat16 [4096, 8192], P('seq', 'head'), may hold values from -6 to 6
- cotangent: bfloat16 [4096, 8192], P('seq', 'head'), may hold values from -6 to 6
- prefix_keys: bfloat16 [4096, 8192], P('seq', 'head'), may hold values from -1.5 to 1.5
- prefix_values: bfloat16 [4096, 8192], P('seq', 'head'), may hold values from -1.5 to 1.5
- gain: float32 [8192], P('head'), may hold values from 0.5 to 1.5
- lengths: int32 [8], P('seq'), may hold values from 64 to 512, as said below
Outputs:
- normed: bfloat16 [4096, 8192], P('seq', 'head')
- query_grad: bfloat16 [4096, 8192], P('seq', 'head')
- key_grad: bfloat16 [4096, 8192], P('seq', 'head')
- value_grad: bfloat16 [4096, 8192], P('seq', 'head')
- prefix_key_grad: bfloat16 [4096, 8192], P('seq', 'head')
- prefix_value_grad: bfloat16 [4096, 8192], P('seq', 'head')
The draws below stay inside these ranges and needn't reach their ends.
Inputs may be any that keep to these rules, and one draw needn't show every extreme that they name: `lengths`: one length per response; some response has exactly 512 live slots and some exactly 64.
All inputs are finite; a program needn't handle non-finite values.
Results may differ from the reference program's by a relative error of at most 0.0058.
Values sent between devices are 32-bit elements; how exact they have to be, the bound alone decides.
A program may use at most 128 MiB of HBM per device.

```python
import jax
import jax.numpy as jnp
from jax import lax

H = 64
HEAD_DIM = 128
BLOCK = 256
RMAX = 512
RESP = 8
PRE = 4096
RTOK = 4096
WIDTH = 8192


def draw_queries(key, part):
    key_head, key_row, key_base = jax.random.split(key, 3)
    col_head = lax.iota(jnp.int32, WIDTH) // HEAD_DIM
    head_factor = jax.random.uniform(key_head, (H,), jnp.float32, 0.8, 1.2)
    head_scale = 10.0 ** (col_head.astype(jnp.float32) / max(H - 1, 1)) * head_factor[col_head]
    row_scale = 10.0 ** jax.random.uniform(key_row, (RTOK, 1), jnp.float32)
    base = jax.random.normal(key_base, (RTOK, WIDTH), jnp.float32)
    return jnp.clip(base * head_scale[None, :] * row_scale, -200.0, 200.0).astype(jnp.bfloat16)


def draw_lengths(key, part):
    key_len, key_shuffle = jax.random.split(key)
    drawn = jax.random.randint(key_len, (RESP,), RMAX // 8, RMAX + 1)
    shuffled = jax.random.permutation(key_shuffle, RESP)
    return drawn.at[shuffled[0]].set(RMAX).at[shuffled[1]].set(RMAX // 8)


def block_scale(key, extent, cuts, low, high):
    loudness = 1.0
    for position, blocks in cuts:
        steps = jax.random.uniform(jax.random.fold_in(jax.random.fold_in(key, 6), position), (blocks,), jnp.float32, low / len(cuts), high / len(cuts))
        loudness = loudness * jnp.repeat(jnp.exp(steps), extent[position] // blocks).reshape((-1,) + (1,) * (len(extent) - 1 - position))
    return loudness


def gaussian(stream_key, dims, scale, reach, shards=(), dtype=jnp.bfloat16):
    level = block_scale(stream_key, dims, shards, -0.22, 0.18) if shards else 1.0
    result = jax.random.normal(stream_key, dims, jnp.float32) * scale * level
    return jnp.minimum(jnp.maximum(result, -reach), reach).astype(dtype)


def setup_inputs(seed: int = 0) -> dict:
    streams_of = jax.random.split(jax.random.key(seed), 9)
    return {
        "queries": draw_queries(jax.random.fold_in(streams_of[8], 71), 0),
        "keys": gaussian(streams_of[1], (RTOK, WIDTH), 1.0, 6.0, ((0, 8), (1, 4))),
        "values": gaussian(streams_of[2], (RTOK, WIDTH), 1.0, 6.0, ((0, 8), (1, 4))),
        "cotangent": gaussian(streams_of[3], (RTOK, WIDTH), 1.0, 6.0, ((0, 8), (1, 4))),
        "prefix_keys": gaussian(streams_of[4], (PRE, WIDTH), 0.25, 1.5, ((0, 8), (1, 4))),
        "prefix_values": gaussian(streams_of[5], (PRE, WIDTH), 0.25, 1.5, ((0, 8), (1, 4))),
        "gain": jnp.clip(1.0 + 0.1 * jax.random.normal(streams_of[6], (WIDTH,), jnp.float32), 0.5, 1.5),
        "lengths": draw_lengths(jax.random.fold_in(streams_of[8], 71), 0),
    }


epsilon = 1e-06

def rounded(value):
    return lax.optimization_barrier(value.astype(jnp.bfloat16)).astype(jnp.float32)

def reference(queries, keys, values, cotangent, prefix_keys, prefix_values, gain, lengths):
    pre_keys = prefix_keys.astype(jnp.float32).reshape(PRE, H, HEAD_DIM)
    pre_values = prefix_values.astype(jnp.float32).reshape(PRE, H, HEAD_DIM)
    prefix_state = jnp.einsum('thd,the->hde', pre_keys, pre_values)
    causal = jnp.tril(jnp.ones((BLOCK, BLOCK), jnp.float32))
    block_count = RMAX // BLOCK

    def respond(pieces):
        q_in, k_in, v_in, cot_in, length = pieces
        live_mask = (jnp.arange(RMAX) < length).astype(jnp.bfloat16)[:, None]

        def shaped(array):
            return (array * live_mask).astype(jnp.float32).reshape(block_count, BLOCK, H, HEAD_DIM)
        q_live = shaped(q_in)
        k_live = shaped(k_in)
        v_live = shaped(v_in)

        def forward(state_now, blocks):
            q_block, k_block, v_block = blocks
            state_bf = rounded(state_now)
            from_state = jnp.einsum('bhd,hde->bhe', q_block, state_bf)
            scores = rounded(jnp.einsum('bhd,shd->hbs', q_block, k_block) * causal)
            in_block = jnp.einsum('hbs,she->bhe', scores, v_block)
            state_next = state_now + jnp.einsum('bhd,bhe->hde', k_block, v_block)
            return (state_next, (from_state + in_block, scores, state_bf))
        final_state, (attended, scores_all, states_all) = lax.scan(forward, prefix_state, (q_live, k_live, v_live))
        attended = attended.reshape(RMAX, WIDTH)
        root_mean = jnp.sqrt(lax.optimization_barrier(jnp.sum(attended * attended, axis=1)) / WIDTH + epsilon)[:, None]
        normed = (gain * attended / root_mean).astype(jnp.bfloat16)
        scaled_cot = gain * (cot_in * live_mask).astype(jnp.float32)
        inner_sum = lax.optimization_barrier(jnp.sum(scaled_cot * attended, axis=1))[:, None]
        out_grad = rounded(scaled_cot / root_mean - attended * inner_sum / (WIDTH * root_mean ** 3))
        out_grad = out_grad.reshape(block_count, BLOCK, H, HEAD_DIM)

        def backward(grad_state, blocks):
            q_block, k_block, v_block, d_block, scores, state_bf = blocks
            grad_bf = rounded(grad_state)
            pscore = rounded(jnp.einsum('bhe,she->hbs', d_block, v_block) * causal)
            grad_q = jnp.einsum('bhe,hde->bhd', d_block, state_bf) + jnp.einsum('hbs,shd->bhd', pscore, k_block)
            grad_k = jnp.einsum('bhe,hde->bhd', v_block, grad_bf) + jnp.einsum('hbs,bhd->shd', pscore, q_block)
            grad_v = jnp.einsum('bhd,hde->bhe', k_block, grad_bf) + jnp.einsum('hbs,bhe->she', scores, d_block)
            grad_next = grad_state + jnp.einsum('bhd,bhe->hde', q_block, d_block)
            return (grad_next, (grad_q, grad_k, grad_v))
        grad_zero = jnp.zeros((H, HEAD_DIM, HEAD_DIM), jnp.float32)
        grad_total, (grad_q, grad_k, grad_v) = lax.scan(backward, grad_zero, (q_live, k_live, v_live, out_grad, scores_all, states_all), reverse=True)
        flat = (normed, grad_q.reshape(RMAX, WIDTH).astype(jnp.bfloat16), grad_k.reshape(RMAX, WIDTH).astype(jnp.bfloat16), grad_v.reshape(RMAX, WIDTH).astype(jnp.bfloat16))
        return (flat, grad_total)
    (normed, query_grad, key_grad, value_grad), state_grads = lax.map(respond, (queries.reshape(RESP, RMAX, WIDTH), keys.reshape(RESP, RMAX, WIDTH), values.reshape(RESP, RMAX, WIDTH), cotangent.reshape(RESP, RMAX, WIDTH), lengths))
    state_grad = lax.optimization_barrier(jnp.sum(state_grads, axis=0))
    prefix_key_grad = jnp.einsum('the,hde->thd', pre_values, state_grad, precision=lax.Precision.HIGHEST).reshape(PRE, WIDTH).astype(jnp.bfloat16)
    prefix_value_grad = jnp.einsum('thd,hde->the', pre_keys, state_grad, precision=lax.Precision.HIGHEST).reshape(PRE, WIDTH).astype(jnp.bfloat16)
    return (normed.reshape(RTOK, WIDTH), query_grad.reshape(RTOK, WIDTH), key_grad.reshape(RTOK, WIDTH), value_grad.reshape(RTOK, WIDTH), prefix_key_grad, prefix_value_grad)
```

```python
import functools

import jax
import jax.numpy as jnp
from jax import lax
from jax.experimental import pallas as pl
from jax.experimental.pallas import tpu as pltpu
from jax.sharding import PartitionSpec as P

HEAD_DIM = 128
BLOCK = 256
EPS = 1e-06
MESH = pl.DeviceIdType.MESH
F32 = jnp.float32
BF16 = jnp.bfloat16
UNIT = 2
SUB = 2
SKEW = 3
STAGES = 2
PLAN = {
    4: (
        ([0, 3, 6, 9], [9, 6, 3, 0], [11, 11, 11, 11], [0, 0, 0, 0]),
        ([0, 3, 6, 9], [9, 6, 3, 0], [11, 11, 11, 11], [0, 0, 0, 0]),
    )
}


def mm(a, b, ca, cb):
    return lax.dot_general(a, b, (((ca,), (cb,)), ((), ())), preferred_element_type=F32)


def timetable(nz, units, ph):
    pieces = units * SUB
    far = SKEW * (nz - 1)
    if nz in PLAN:
        right, left, other, work = PLAN[nz][ph]
    else:
        right = [SKEW * k for k in range(nz)]
        left = [SKEW * (nz - 1 - k) for k in range(nz)]
        other, work = [far + SUB] * nz, [0] * nz
    rows = []
    for k in range(nz):
        own = max(right[k], left[k], work[k] + STAGES - SUB)
        oth = max(other[k], own, work[k] + (units + 1) * STAGES - SUB)
        last = max(pieces + own, pieces + oth, work[k] + 2 * units * STAGES)
        rows.append((right[k], left[k], own, oth, work[k], last))
    return rows


def kernel(nh, ns, width, *refs):
    (q_hbm, k_hbm, v_hbm, dy_hbm, pk_hbm, pv_hbm, gain_hbm, len_ref) = refs[:8]
    stage = refs[8:12]
    pk, pv, tout = refs[12:15]
    (q, k, v, dy, do, o, sc, ps, kv, mb, gb, sq, inn, rinv, coef) = refs[15:30]
    st_out, st_in = refs[30:32]
    bufs = (refs[32:41], refs[41:50])
    in_sem, st_send, st_recv, send_sem, recv_sem, gain_ref = refs[50:56]

    rows, cols = q.shape
    heads = cols // HEAD_DIM
    nown = heads // 2
    units = nown // UNIT
    nb = rows // BLOCK
    nz = ns // 2
    me_h = lax.axis_index("head")
    me_s = lax.axis_index("seq")
    z = me_s // 2
    core = me_s % 2
    own0 = core * nown
    oth0 = (1 - core) * nown
    partner = (me_h, z * 2 + 1 - core)
    right = (me_h, jnp.minimum(me_s + 2, ns - 1))
    left = (me_h, jnp.maximum(me_s - 2, 0))
    not_first = z > 0
    not_last = z < nz - 1

    def cs(h):
        return pl.ds(pl.multiple_of(h * HEAD_DIM, HEAD_DIM), HEAD_DIM)

    def part(j, src, dst, head, count):
        c = pl.ds(pl.multiple_of(head * HEAD_DIM, HEAD_DIM), count * HEAD_DIM)
        return pltpu.make_async_copy(src.at[:, c], dst.at[:, c], in_sem.at[j])

    loads = [
        part(0, pk_hbm, pk, oth0, UNIT),
        part(1, pv_hbm, pv, oth0, UNIT),
        part(2, pk_hbm, pk, oth0 + UNIT, nown - UNIT),
        part(3, pv_hbm, pv, oth0 + UNIT, nown - UNIT),
        part(4, pk_hbm, pk, own0, nown),
        part(5, pv_hbm, pv, own0, nown),
        pltpu.make_async_copy(q_hbm, q, in_sem.at[6]),
        pltpu.make_async_copy(k_hbm, k, in_sem.at[7]),
        pltpu.make_async_copy(v_hbm, v, in_sem.at[8]),
        pltpu.make_async_copy(dy_hbm, dy, in_sem.at[9]),
        pltpu.make_async_copy(gain_hbm, gain_ref, in_sem.at[10]),
    ]
    for c in loads[:6]:
        c.start()

    barrier = pltpu.get_barrier_semaphore()
    pl.semaphore_signal(barrier, inc=1, device_id=partner, device_id_type=MESH)

    @pl.when(not_first)
    def _():
        pl.semaphore_signal(barrier, inc=1, device_id=left, device_id_type=MESH)

    @pl.when(not_last)
    def _():
        pl.semaphore_signal(barrier, inc=1, device_id=right, device_id_type=MESH)

    for d in range(1, nh):
        pl.semaphore_signal(
            barrier, inc=1, device_id=((me_h + d) % nh, me_s), device_id_type=MESH
        )

    sq[...] = jnp.zeros_like(sq)
    inn[...] = jnp.zeros_like(inn)
    for c in loads[:2]:
        c.wait()
    for c in loads[6:]:
        c.start()

    def causal():
        r = lax.broadcasted_iota(jnp.int32, (BLOCK, BLOCK), 0)
        c = lax.broadcasted_iota(jnp.int32, (BLOCK, BLOCK), 1)
        return r >= c

    def pick(values):
        found = jnp.int32(0)
        for k, value in enumerate(values):
            found = found + (z == k).astype(jnp.int32) * value
        return found

    plans = [timetable(nz, units, ph) for ph in range(2)]

    def exchange(ph, produce, compute, consume, ready):
        xo, xi, x, rin, rout, lin, lout, tot, tin = bufs[ph]
        pieces = units * SUB

        def hop(kind, src, dst, i, dev):
            return pltpu.make_async_remote_copy(
                src_ref=src,
                dst_ref=dst,
                send_sem=send_sem.at[ph, kind],
                recv_sem=recv_sem.at[ph, kind, i],
                device_id=dev,
                device_id_type=MESH,
            )

        def to_partner(u):
            return hop(0, xo.at[u], xi.at[u], u, partner)

        def total_out(i):
            return hop(1, tot.at[i // SUB, i % SUB], tin.at[i // SUB, i % SUB], i, partner)

        def to_right(i):
            return hop(2, rout.at[i // SUB, i % SUB], rin.at[i // SUB, i % SUB], i, right)

        def to_left(i):
            return hop(3, lout.at[i // SUB, i % SUB], lin.at[i // SUB, i % SUB], i, left)

        def make(dst, u, first):
            for j, state in enumerate(produce(first + u * UNIT)):
                per = SUB // UNIT
                dst[u, j * per : (j + 1) * per] = state.reshape(per, -1, HEAD_DIM)

        def give(u):
            make(xo, u, oth0)
            to_partner(u).start()

        def states(ref, u):
            per = SUB // UNIT
            return [
                ref[u, j * per : (j + 1) * per].reshape(HEAD_DIM, HEAD_DIM) for j in range(UNIT)
            ]

        make(xo, 0, oth0)
        ready(-2)
        to_partner(0).start()
        ready(-1)
        plan = [pick([p[j] for p in plans[ph]]) for j in range(6)]
        r_at, l_at, t_at, o_at, c_at, slots = plan

        def slot(s, carry):
            u = s // SUB
            fresh = s % SUB == 0

            @pl.when(fresh & (u + 1 < units))
            def _():
                give(u + 1)

            @pl.when(fresh & (u < units))
            def _():
                make(x, u, own0)
                to_partner(u).wait_recv()
                x[u] = x[u] + xi[u]

            i_r = s - r_at

            @pl.when((i_r >= 0) & (i_r < pieces))
            def _():
                i, j = i_r // SUB, i_r % SUB

                @pl.when(not_first)
                def _():
                    to_right(i_r).wait_recv()
                    rout[i, j] = rin[i, j] + x[i, j]

                @pl.when(jnp.logical_not(not_first))
                def _():
                    rout[i, j] = x[i, j]

                @pl.when(not_last)
                def _():
                    to_right(i_r).start()

            i_l = s - l_at

            @pl.when((i_l >= 0) & (i_l < pieces))
            def _():
                i, j = i_l // SUB, i_l % SUB

                @pl.when(not_last)
                def _():
                    to_left(i_l).wait_recv()
                    lout[i, j] = lin[i, j] + x[i, j]

                @pl.when(jnp.logical_not(not_last))
                def _():
                    lout[i, j] = x[i, j]

                @pl.when(not_first)
                def _():
                    to_left(i_l).start()

            i_t = s - t_at

            @pl.when((i_t >= 0) & (i_t < pieces))
            def _():
                i, j = i_t // SUB, i_t % SUB

                @pl.when(not_last)
                def _():
                    tot[i, j] = rout[i, j] + lin[i, j]

                @pl.when(jnp.logical_not(not_last))
                def _():
                    tot[i, j] = rout[i, j]

                total_out(i_t).start()

            work = s - c_at
            ready(work)

            @pl.when((work >= 0) & (work < 2 * units * STAGES))
            def _():
                h = (own0 + work // STAGES * UNIT) % heads
                for c in range(STAGES):

                    @pl.when(work % STAGES == c)
                    def _(c=c):
                        compute[c](h)

            @pl.when((i_t >= 0) & (i_t < pieces) & (i_t % SUB == SUB - 1))
            def _():
                i = i_t // SUB
                consume(own0 + i * UNIT, states(tot, i))

            i_o = s - o_at

            @pl.when((i_o >= 0) & (i_o < pieces) & (i_o % SUB == SUB - 1))
            def _():
                i = i_o // SUB
                for j in range(SUB):
                    total_out(i * SUB + j).wait_recv()
                consume(oth0 + i * UNIT, states(tin, i))

            return carry

        lax.fori_loop(0, slots, slot, 0)

        hop(0, xo, xi, 0, partner).wait_send()
        hop(1, tot, tin, 0, partner).wait_send()

        @pl.when(not_last)
        def _():
            hop(2, rout, rin, 0, right).wait_send()

        @pl.when(not_first)
        def _():
            hop(3, lout, lin, 0, left).wait_send()

    def blk(ref, c, h):
        return ref[pl.ds(c * BLOCK, BLOCK), cs(h)]

    def prefix_part(h):
        return [mm(pk[:, cs(h + j)], pv[:, cs(h + j)], 0, 0) for j in range(UNIT)]

    items = [(j, c) for j in range(UNIT) for c in range(nb)]

    def score(h):
        seen = causal()
        for j, c in items:
            a = mm(blk(q, c, h + j), blk(k, c, h + j), 1, 1)
            sc[h + j, c] = jnp.where(seen, a, 0.0).astype(BF16)

    def attend(h):
        for j, c in items:
            vc = blk(v, c, h + j)
            o[pl.ds(c * BLOCK, BLOCK), cs(h + j)] = mm(sc[h + j, c], vc, 1, 0)
            if c < nb - 1:
                add = mm(blk(k, c, h + j), vc, 0, 0)
                kv[h + j, c] = add if c == 0 else kv[h + j, c - 1] + add

    def loaded(s):
        if isinstance(s, int):
            if s == -2:
                pl.semaphore_wait(
                    barrier, nh + not_first.astype(jnp.int32) + not_last.astype(jnp.int32)
                )
            else:
                for c in loads[2:6]:
                    c.wait()
            return

        @pl.when(s == 0)
        def _():
            for c in loads[6:9]:
                c.wait()

        @pl.when(s == 1)
        def _():
            loads[9].wait()
            loads[10].wait()

    def use_state(h, got):
        for c in range(nb):
            r = pl.ds(c * BLOCK, BLOCK)
            squares, inner = sq[r, :], inn[r, :]
            for j, state in enumerate(got):
                st = (state if c == 0 else state + kv[h + j, c - 1]).astype(BF16)
                mb[h + j, c] = st
                oc = o[r, cs(h + j)] + mm(blk(q, c, h + j), st, 1, 0)
                o[r, cs(h + j)] = oc
                squares = squares + oc * oc
                inner = inner + blk(dy, c, h + j).astype(F32) * gain_ref[:, cs(h + j)] * oc
            sq[r, :] = squares
            inn[r, :] = inner

    exchange(0, prefix_part, (score, attend), use_state, loaded)

    row_sq = jnp.sum(sq[...].T, axis=0, keepdims=True)
    row_in = jnp.sum(inn[...].T, axis=0, keepdims=True)
    lanes = rows // HEAD_DIM

    def fold(row):
        return [row[:, i * HEAD_DIM : (i + 1) * HEAD_DIM] for i in range(lanes)]

    def unfold(tile, first):
        return jnp.concatenate([tile[first + i : first + i + 1] for i in range(lanes)], axis=1)

    st_out[...] = jnp.concatenate(fold(row_sq) + fold(row_in), axis=0)
    copies = []
    for d in range(1, nh):
        copies.append(
            pltpu.make_async_remote_copy(
                src_ref=st_out,
                dst_ref=st_in.at[d - 1],
                send_sem=st_send.at[d - 1],
                recv_sem=st_recv.at[d - 1],
                device_id=((me_h + d) % nh, me_s),
                device_id_type=MESH,
            )
        )
        copies[-1].start()
    total = st_out[...]
    for d in range(1, nh):
        copies[d - 1].wait_recv()
        total = total + st_in[d - 1]
    inv = 1.0 / jnp.sqrt(unfold(total, 0) / width + EPS)
    cf = unfold(total, lanes) * (inv * inv * inv) / width
    live = lax.broadcasted_iota(jnp.int32, (1, rows), 1) < len_ref[0]
    inv = jnp.where(live, inv, 0.0)
    cf = jnp.where(live, cf, 0.0)
    rinv[...] = jnp.broadcast_to(inv, (HEAD_DIM, rows)).T
    coef[...] = jnp.broadcast_to(cf, (HEAD_DIM, rows)).T

    def state_grad(h):
        run = [None] * UNIT
        for c in reversed(range(nb)):
            r = pl.ds(c * BLOCK, BLOCK)
            ri, cf = rinv[r, :], coef[r, :]
            for j in range(UNIT):
                g = gain_ref[:, cs(h + j)]
                oc = o[r, cs(h + j)]
                stage[0][r, cs(h + j)] = (g * oc * ri).astype(BF16)
                d = (blk(dy, c, h + j).astype(F32) * g * ri - oc * cf).astype(BF16)
                do[r, cs(h + j)] = d
                if c < nb - 1:
                    gb[h + j, c] = run[j].astype(BF16)
                part = mm(blk(q, c, h + j), d, 0, 0)
                run[j] = part if run[j] is None else run[j] + part
        return run

    def query_side(h):
        seen = causal()
        for j, c in items:
            dc = blk(do, c, h + j)
            p = jnp.where(seen, mm(dc, blk(v, c, h + j), 1, 1), 0.0).astype(BF16)
            ps[0, j, c] = p
            qg = mm(dc, mb[h + j, c], 1, 1) + mm(p, blk(k, c, h + j), 1, 0)
            stage[1][pl.ds(c * BLOCK, BLOCK), cs(h + j)] = qg.astype(BF16)

    def key_side(h):
        for j, c in items:
            r = pl.ds(c * BLOCK, BLOCK)
            kg = mm(ps[0, j, c], blk(q, c, h + j), 0, 0)
            vg = mm(sc[h + j, c], blk(do, c, h + j), 0, 0)
            if c < nb - 1:
                g = gb[h + j, c]
                kg = kg + mm(blk(v, c, h + j), g, 1, 1)
                vg = vg + mm(blk(k, c, h + j), g, 1, 0)
            stage[2][r, cs(h + j)] = kg.astype(BF16)
            stage[3][r, cs(h + j)] = vg.astype(BF16)

    def keep_total(h, got):
        for j, state in enumerate(got):
            tout[h + j] = state

    exchange(1, state_grad, (query_side, key_side), keep_total, lambda s: None)
    for c in copies:
        c.wait_send()


def finish(*refs):
    ready = refs[:4]
    pk, pv, total = refs[4:7]
    outs = refs[7:13]
    pkg, pvg, sem = refs[13:16]
    heads = total.shape[0]
    for j in range(4):
        pltpu.make_async_copy(ready[j], outs[j], sem.at[j]).start()

    def head(h, carry):
        c = pl.ds(pl.multiple_of(h * HEAD_DIM, HEAD_DIM), HEAD_DIM)
        state = total[h]
        hi = state.astype(BF16)
        lo = (state - hi.astype(F32)).astype(BF16)
        vals, keys = pv[:, c], pk[:, c]
        vv = jnp.concatenate([vals, vals], axis=1)
        kk = jnp.concatenate([keys, keys], axis=1)
        pkg[:, c] = mm(vv, jnp.concatenate([hi, lo], axis=1), 1, 1).astype(BF16)
        pvg[:, c] = mm(kk, jnp.concatenate([hi, lo], axis=0), 1, 0).astype(BF16)
        pltpu.make_async_copy(pkg.at[:, c], outs[4].at[:, c], sem.at[4]).start()
        pltpu.make_async_copy(pvg.at[:, c], outs[5].at[:, c], sem.at[5]).start()
        return carry

    lax.fori_loop(0, heads, head, 0)
    for j in range(4):
        pltpu.make_async_copy(ready[j], outs[j], sem.at[j]).wait()
    pltpu.make_async_copy(pkg, outs[4], sem.at[4]).wait()
    pltpu.make_async_copy(pvg, outs[5], sem.at[5]).wait()


def body(nh, ns, queries, keys, values, cotangent, prefix_keys, prefix_values, gain, lengths):
    rows, cols = queries.shape
    heads = cols // HEAD_DIM
    nown = heads // 2
    nb = rows // BLOCK
    any_spec = pl.BlockSpec(memory_space=pl.ANY)
    big = pltpu.VMEM((rows, cols), BF16)
    row = pltpu.VMEM((rows, HEAD_DIM), F32)
    units = nown // UNIT
    states = [pltpu.VMEM((units, SUB, UNIT * HEAD_DIM // SUB, HEAD_DIM), F32)] * 9
    scratch = (
        [big] * 5
        + [
            pltpu.VMEM((rows, cols), F32),
            pltpu.VMEM((heads, nb, BLOCK, BLOCK), BF16),
            pltpu.VMEM((1, UNIT, nb, BLOCK, BLOCK), BF16),
            pltpu.VMEM((heads, max(nb - 1, 1), HEAD_DIM, HEAD_DIM), F32),
            pltpu.VMEM((heads, nb, HEAD_DIM, HEAD_DIM), BF16),
            pltpu.VMEM((heads, max(nb - 1, 1), HEAD_DIM, HEAD_DIM), BF16),
            row,
            row,
            row,
            row,
        ]
        + [
            pltpu.VMEM((2 * rows // HEAD_DIM, HEAD_DIM), F32),
            pltpu.VMEM((max(nh - 1, 1), 2 * rows // HEAD_DIM, HEAD_DIM), F32),
        ]
        + states
        + states
        + [
            pltpu.SemaphoreType.DMA((11,)),
            pltpu.SemaphoreType.DMA((max(nh - 1, 1),)),
            pltpu.SemaphoreType.DMA((max(nh - 1, 1),)),
            pltpu.SemaphoreType.DMA((2, 4)),
            pltpu.SemaphoreType.DMA((2, 4, units * SUB)),
            pltpu.VMEM((1, cols), F32),
        ]
    )
    fast = pl.BlockSpec(memory_space=pltpu.VMEM)
    tot = pltpu.VMEM((heads, HEAD_DIM, HEAD_DIM), F32)
    wide = [queries, keys, values, cotangent, prefix_keys, prefix_values]
    wide.append(gain.reshape(1, cols))
    wide = [pltpu.with_memory_space_constraint(x, pltpu.HBM) for x in wide]
    made = pl.pallas_call(
        functools.partial(kernel, nh, ns, float(cols * nh)),
        out_shape=[big] * 6 + [tot],
        in_specs=[any_spec] * 7 + [pl.BlockSpec(memory_space=pltpu.SMEM)],
        out_specs=[fast] * 7,
        scratch_shapes=scratch,
        compiler_params=pltpu.CompilerParams(
            collective_id=0, has_side_effects=True, vmem_limit_bytes=38 * 1024 * 1024
        ),
    )(*wide, lengths)
    made = [pltpu.with_memory_space_constraint(x, pltpu.VMEM) for x in made]
    out = pltpu.HBM((rows, cols), BF16)
    return tuple(
        pl.pallas_call(
            finish,
            out_shape=[out] * 6,
            in_specs=[fast] * 7,
            out_specs=[any_spec] * 6,
            scratch_shapes=[big, big, pltpu.SemaphoreType.DMA((6,))],
            compiler_params=pltpu.CompilerParams(vmem_limit_bytes=8 * 1024 * 1024),
        )(*made)
    )


def solution(mesh):
    nh, ns = mesh.shape["head"], mesh.shape["seq"]
    tok = P("seq", "head")
    return jax.shard_map(
        functools.partial(body, nh, ns),
        mesh=mesh,
        in_specs=(tok,) * 6 + (P("head"), P("seq")),
        out_specs=(tok,) * 6,
        check_vma=False,
    )
```

```python
import functools

import jax
import jax.numpy as jnp
from jax import lax
from jax.experimental import pallas as pl
from jax.experimental.pallas import tpu as pltpu
from jax.sharding import PartitionSpec as P

HEAD_DIM = 128
BLOCK = 256
EPS = 1e-06
MESH = pl.DeviceIdType.MESH
F32 = jnp.float32
BF16 = jnp.bfloat16
UNIT = 2
SUB = 2
SKEW = 3
STAGES = 2
AHEAD = 2
GROUP = 4
PLAN = {
    4: (
        ([0, 3, 6, 9], [9, 6, 3, 0], [10, 7, 7, 10], [(4, 2, 1, 16, 99, 1, 1), (2, 1, 1, 16, 99, 1, 1), (2, 1, 1, 16, 99, 1, 1), (4, 2, 1, 16, 99, 1, 1)]),
        ([0, 3, 6, 9], [9, 6, 3, 0], [10, 7, 7, 10], [(4, 2, 1, 10, 9, 1, 1), (2, 1, 1, 16, 99, 1, 1), (2, 1, 1, 16, 99, 1, 1), (4, 2, 1, 10, 9, 1, 1)]),
    )
}


def mm(a, b, ca, cb):
    return lax.dot_general(a, b, (((ca,), (cb,)), ((), ())), preferred_element_type=F32)


def clip(value, top):
    if isinstance(value, int):
        return min(max(value, 0), top)
    return jnp.minimum(jnp.maximum(value, 0), top)


def done_by(s, row, total):
    first, up, down, count, second, up2, down2 = row
    fast = clip((s + 1 - first) * up // down, count)
    return fast + clip((s + 1 - second) * up2 // down2, total - count)


def timetable(nz, units, ph):
    pieces = units * SUB
    total = 2 * units * STAGES
    if nz in PLAN:
        right, left, other, work = PLAN[nz][ph]
    else:
        right = [SKEW * k for k in range(nz)]
        left = [SKEW * (nz - 1 - k) for k in range(nz)]
        other, work = [SKEW * (nz - 1) + SUB] * nz, [(2, 1, 1, total, 0, 1, 1)] * nz
    rows = []
    for k in range(nz):
        own = max(right[k], left[k])
        while any(
            done_by(u * SUB + own, work[k], total) < (u + 1) * STAGES
            for u in range(units)
        ):
            own += 1
        oth = max(other[k], own)
        while any(
            done_by(u * SUB + oth, work[k], total) < (units + u + 1) * STAGES
            for u in range(units)
        ):
            oth += 1
        last = pieces + oth
        while done_by(last - 1, work[k], total) < total:
            last += 1
        rows.append((right[k], left[k], own, oth, last) + tuple(work[k]))
    return rows


def kernel(nh, ns, width, *refs):
    (q_hbm, k_hbm, v_hbm, dy_hbm, pk_hbm, pv_hbm, gain_hbm, len_ref) = refs[:8]
    stage = refs[8:12]
    pk, pv, tout = refs[12:15]
    (q, k, v, dy, do, o, sc, ps, kv, mb, gb, sq, inn, rinv, coef) = refs[15:30]
    st_out, st_in = refs[30:32]
    bufs = (refs[32:41], refs[41:50])
    in_sem, st_send, st_recv, send_sem, recv_sem, gain_ref = refs[50:56]

    rows, cols = q.shape
    heads = cols // HEAD_DIM
    nown = heads // 2
    units = nown // UNIT
    nb = rows // BLOCK
    nz = ns // 2
    me_h = lax.axis_index("head")
    me_s = lax.axis_index("seq")
    z = me_s // 2
    core = me_s % 2
    own0 = core * nown
    oth0 = (1 - core) * nown
    partner = (me_h, z * 2 + 1 - core)
    right = (me_h, jnp.minimum(me_s + 2, ns - 1))
    left = (me_h, jnp.maximum(me_s - 2, 0))
    not_first = z > 0
    not_last = z < nz - 1

    def cs(h):
        return pl.ds(pl.multiple_of(h * HEAD_DIM, HEAD_DIM), HEAD_DIM)

    def part(j, src, dst, head, count):
        c = pl.ds(pl.multiple_of(head * HEAD_DIM, HEAD_DIM), count * HEAD_DIM)
        return pltpu.make_async_copy(src.at[:, c], dst.at[:, c], in_sem.at[j])

    loads = [
        part(0, pk_hbm, pk, oth0, UNIT),
        part(1, pv_hbm, pv, oth0, UNIT),
        part(2, pk_hbm, pk, own0, UNIT),
        part(3, pv_hbm, pv, own0, UNIT),
        part(4, pk_hbm, pk, oth0 + UNIT, nown - UNIT),
        part(5, pv_hbm, pv, oth0 + UNIT, nown - UNIT),
        part(6, pk_hbm, pk, own0 + UNIT, nown - UNIT),
        part(7, pv_hbm, pv, own0 + UNIT, nown - UNIT),
        pltpu.make_async_copy(q_hbm, q, in_sem.at[8]),
        pltpu.make_async_copy(k_hbm, k, in_sem.at[9]),
        pltpu.make_async_copy(v_hbm, v, in_sem.at[10]),
        pltpu.make_async_copy(dy_hbm, dy, in_sem.at[11]),
        pltpu.make_async_copy(gain_hbm, gain_ref, in_sem.at[12]),
    ]
    for c in loads[:8]:
        c.start()

    barrier = pltpu.get_barrier_semaphore()
    pl.semaphore_signal(barrier, inc=1, device_id=partner, device_id_type=MESH)

    @pl.when(not_first)
    def _():
        pl.semaphore_signal(barrier, inc=1, device_id=left, device_id_type=MESH)

    @pl.when(not_last)
    def _():
        pl.semaphore_signal(barrier, inc=1, device_id=right, device_id_type=MESH)

    for d in range(1, nh):
        pl.semaphore_signal(
            barrier, inc=1, device_id=((me_h + d) % nh, me_s), device_id_type=MESH
        )

    sq[...] = jnp.zeros_like(sq)
    inn[...] = jnp.zeros_like(inn)
    for c in loads[:2]:
        c.wait()
    for c in loads[8:]:
        c.start()

    def causal():
        r = lax.broadcasted_iota(jnp.int32, (BLOCK, BLOCK), 0)
        c = lax.broadcasted_iota(jnp.int32, (BLOCK, BLOCK), 1)
        return r >= c

    def pick(values):
        found = jnp.int32(0)
        for k, value in enumerate(values):
            found = found + (z == k).astype(jnp.int32) * value
        return found

    plans = [timetable(nz, units, ph) for ph in range(2)]

    def exchange(ph, produce, compute, consume, ready, more):
        xo, xi, x, rin, rout, lin, lout, tot, tin = bufs[ph]
        pieces = units * SUB

        def hop(kind, src, dst, i, dev):
            return pltpu.make_async_remote_copy(
                src_ref=src,
                dst_ref=dst,
                send_sem=send_sem.at[ph, kind],
                recv_sem=recv_sem.at[ph, kind, i],
                device_id=dev,
                device_id_type=MESH,
            )

        def to_partner(u):
            return hop(0, xo.at[u], xi.at[u], u, partner)

        def total_out(i):
            return hop(1, tot.at[i // SUB, i % SUB], tin.at[i // SUB, i % SUB], i, partner)

        def to_right(i):
            return hop(2, rout.at[i // SUB, i % SUB], rin.at[i // SUB, i % SUB], i, right)

        def to_left(i):
            return hop(3, lout.at[i // SUB, i % SUB], lin.at[i // SUB, i % SUB], i, left)

        def make(dst, u, first):
            for j, state in enumerate(produce(first + u * UNIT)):
                per = SUB // UNIT
                dst[u, j * per : (j + 1) * per] = state.reshape(per, -1, HEAD_DIM)

        def give(u):
            make(xo, u, oth0)
            to_partner(u).start()

        def state_of(ref, i):
            per = SUB // UNIT
            first = i % UNIT * per
            return ref[i // UNIT, pl.ds(first, per)].reshape(HEAD_DIM, HEAD_DIM)

        make(xo, 0, oth0)
        ready(-2)
        to_partner(0).start()
        ready(-1)
        plan = [pick([p[j] for p in plans[ph]]) for j in range(12)]
        r_at, l_at, t_at, o_at, slots = plan[:5]
        total = 2 * units * STAGES

        def slot(s, carry):
            u = s // SUB
            fresh = s % SUB == 0

            @pl.when(fresh & (u < units))
            def _():
                make(x, u, own0)
                to_partner(u).wait_recv()
                x[u] = x[u] + xi[u]

            i_r = s - r_at

            @pl.when((i_r >= 0) & (i_r < pieces))
            def _():
                i, j = i_r // SUB, i_r % SUB

                @pl.when(not_first)
                def _():
                    to_right(i_r).wait_recv()
                    rout[i, j] = rin[i, j] + x[i, j]

                @pl.when(jnp.logical_not(not_first))
                def _():
                    rout[i, j] = x[i, j]

                @pl.when(not_last)
                def _():
                    to_right(i_r).start()

            i_l = s - l_at

            @pl.when((i_l >= 0) & (i_l < pieces))
            def _():
                i, j = i_l // SUB, i_l % SUB

                @pl.when(not_last)
                def _():
                    to_left(i_l).wait_recv()
                    lout[i, j] = lin[i, j] + x[i, j]

                @pl.when(jnp.logical_not(not_last))
                def _():
                    lout[i, j] = x[i, j]

                @pl.when(not_first)
                def _():
                    to_left(i_l).start()

            more(s)

            @pl.when(s == 0)
            def _():
                for ahead in range(1, min(AHEAD, units)):
                    give(ahead)

            @pl.when(fresh & (u + AHEAD < units))
            def _():
                give(u + AHEAD)

            i_t = s - t_at

            @pl.when((i_t >= 0) & (i_t < pieces))
            def _():
                i, j = i_t // SUB, i_t % SUB

                @pl.when(not_last)
                def _():
                    tot[i, j] = rout[i, j] + lin[i, j]

                @pl.when(jnp.logical_not(not_last))
                def _():
                    tot[i, j] = rout[i, j]

                total_out(i_t).start()

            def chunk(w, carry):
                ready(w)
                h = (own0 + w // STAGES * UNIT) % heads
                for c in range(STAGES):

                    @pl.when(w % STAGES == c)
                    def _(c=c):
                        compute[c](h)

                return carry

            lax.fori_loop(done_by(s - 1, plan[5:], total), done_by(s, plan[5:], total), chunk, 0)

            per = SUB // UNIT

            @pl.when((i_t >= 0) & (i_t < pieces) & (i_t % per == per - 1))
            def _():
                consume(own0 + i_t // per, state_of(tot, i_t // per))

            i_o = s - o_at

            @pl.when((i_o >= 0) & (i_o < pieces) & (i_o % per == per - 1))
            def _():
                for j in range(per):
                    total_out(i_o // per * per + j).wait_recv()
                consume(oth0 + i_o // per, state_of(tin, i_o // per))

            return carry

        lax.fori_loop(0, slots, slot, 0)

        hop(0, xo, xi, 0, partner).wait_send()
        hop(1, tot, tin, 0, partner).wait_send()

        @pl.when(not_last)
        def _():
            hop(2, rout, rin, 0, right).wait_send()

        @pl.when(not_first)
        def _():
            hop(3, lout, lin, 0, left).wait_send()

    def blk(ref, c, h):
        return ref[pl.ds(c * BLOCK, BLOCK), cs(h)]

    def prefix_part(h):
        return [mm(pk[:, cs(h + j)], pv[:, cs(h + j)], 0, 0) for j in range(UNIT)]

    items = [(j, c) for j in range(UNIT) for c in range(nb)]

    def score(h):
        seen = causal()
        for j, c in items:
            a = mm(blk(q, c, h + j), blk(k, c, h + j), 1, 1)
            sc[h + j, c] = jnp.where(seen, a, 0.0).astype(BF16)

    def attend(h):
        for j, c in items:
            vc = blk(v, c, h + j)
            o[pl.ds(c * BLOCK, BLOCK), cs(h + j)] = mm(sc[h + j, c], vc, 1, 0)
            if c < nb - 1:
                add = mm(blk(k, c, h + j), vc, 0, 0)
                kv[h + j, c] = add if c == 0 else kv[h + j, c - 1] + add

    def loaded(s):
        if isinstance(s, int):
            if s == -2:
                pl.semaphore_wait(
                    barrier, nh + not_first.astype(jnp.int32) + not_last.astype(jnp.int32)
                )
            else:
                for c in loads[2:4]:
                    c.wait()
            return

        @pl.when(s == 0)
        def _():
            for c in loads[8:11]:
                c.wait()

        @pl.when(s == 1)
        def _():
            loads[11].wait()
            loads[12].wait()

    def loaded_rest(s):
        @pl.when(s == 0)
        def _():
            for c in loads[4:8]:
                c.wait()

    def use_state(h, state):
        g = gain_ref[:, cs(h)]
        for c in range(nb):
            r = pl.ds(c * BLOCK, BLOCK)
            st = (state if c == 0 else state + kv[h, c - 1]).astype(BF16)
            mb[h, c] = st
            oc = o[r, cs(h)] + mm(blk(q, c, h), st, 1, 0)
            o[r, cs(h)] = oc
            sq[r, :] += oc * oc
            inn[r, :] += blk(dy, c, h).astype(F32) * g * oc

    exchange(0, prefix_part, (score, attend), use_state, loaded, loaded_rest)

    row_sq = jnp.sum(sq[...].T, axis=0, keepdims=True)
    row_in = jnp.sum(inn[...].T, axis=0, keepdims=True)
    lanes = rows // HEAD_DIM

    def fold(row):
        return [row[:, i * HEAD_DIM : (i + 1) * HEAD_DIM] for i in range(lanes)]

    def unfold(tile, first):
        return jnp.concatenate([tile[first + i : first + i + 1] for i in range(lanes)], axis=1)

    st_out[...] = jnp.concatenate(fold(row_sq) + fold(row_in), axis=0)
    copies = []
    for d in range(1, nh):
        copies.append(
            pltpu.make_async_remote_copy(
                src_ref=st_out,
                dst_ref=st_in.at[d - 1],
                send_sem=st_send.at[d - 1],
                recv_sem=st_recv.at[d - 1],
                device_id=((me_h + d) % nh, me_s),
                device_id_type=MESH,
            )
        )
        copies[-1].start()
    total = st_out[...]
    for d in range(1, nh):
        copies[d - 1].wait_recv()
        total = total + st_in[d - 1]
    inv = 1.0 / jnp.sqrt(unfold(total, 0) / width + EPS)
    cf = unfold(total, lanes) * (inv * inv * inv) / width
    live = lax.broadcasted_iota(jnp.int32, (1, rows), 1) < len_ref[0]
    inv = jnp.where(live, inv, 0.0)
    cf = jnp.where(live, cf, 0.0)
    rinv[...] = jnp.broadcast_to(inv, (HEAD_DIM, rows)).T
    coef[...] = jnp.broadcast_to(cf, (HEAD_DIM, rows)).T

    def state_grad(h):
        run = [None] * UNIT
        for c in reversed(range(nb)):
            r = pl.ds(c * BLOCK, BLOCK)
            ri, cf = rinv[r, :], coef[r, :]
            for j in range(UNIT):
                g = gain_ref[:, cs(h + j)]
                oc = o[r, cs(h + j)]
                stage[0][r, cs(h + j)] = (g * oc * ri).astype(BF16)
                d = (blk(dy, c, h + j).astype(F32) * g * ri - oc * cf).astype(BF16)
                do[r, cs(h + j)] = d
                if c < nb - 1:
                    gb[h + j, c] = run[j].astype(BF16)
                part = mm(blk(q, c, h + j), d, 0, 0)
                run[j] = part if run[j] is None else run[j] + part
        return run

    def query_side(h):
        seen = causal()
        for j, c in items:
            dc = blk(do, c, h + j)
            p = jnp.where(seen, mm(dc, blk(v, c, h + j), 1, 1), 0.0).astype(BF16)
            ps[0, j, c] = p
            qg = mm(dc, mb[h + j, c], 1, 1) + mm(p, blk(k, c, h + j), 1, 0)
            stage[1][pl.ds(c * BLOCK, BLOCK), cs(h + j)] = qg.astype(BF16)

    def key_side(h):
        for j, c in items:
            r = pl.ds(c * BLOCK, BLOCK)
            kg = mm(ps[0, j, c], blk(q, c, h + j), 0, 0)
            vg = mm(sc[h + j, c], blk(do, c, h + j), 0, 0)
            if c < nb - 1:
                g = gb[h + j, c]
                kg = kg + mm(blk(v, c, h + j), g, 1, 1)
                vg = vg + mm(blk(k, c, h + j), g, 1, 0)
            stage[2][r, cs(h + j)] = kg.astype(BF16)
            stage[3][r, cs(h + j)] = vg.astype(BF16)

    def keep_total(h, state):
        tout[h] = state

    exchange(1, state_grad, (query_side, key_side), keep_total, lambda s: None, lambda s: None)
    for c in copies:
        c.wait_send()


def finish(*refs):
    ready = refs[:4]
    pk, pv, total = refs[4:7]
    outs = refs[7:13]
    pkg, pvg, sem = refs[13:16]
    heads = total.shape[0]
    for j in range(4):
        pltpu.make_async_copy(ready[j], outs[j], sem.at[j]).start()

    def some(i, carry):
        for j in range(GROUP):
            h = i * GROUP + j
            c = pl.ds(pl.multiple_of(h * HEAD_DIM, HEAD_DIM), HEAD_DIM)
            state = total[h]
            hi = state.astype(BF16)
            lo = (state - hi.astype(F32)).astype(BF16)
            vals, keys = pv[:, c], pk[:, c]
            vv = jnp.concatenate([vals, vals], axis=1)
            kk = jnp.concatenate([keys, keys], axis=1)
            pkg[:, c] = mm(vv, jnp.concatenate([hi, lo], axis=1), 1, 1).astype(BF16)
            pvg[:, c] = mm(kk, jnp.concatenate([hi, lo], axis=0), 1, 0).astype(BF16)
        c = pl.ds(pl.multiple_of(i * GROUP * HEAD_DIM, HEAD_DIM), GROUP * HEAD_DIM)
        pltpu.make_async_copy(pkg.at[:, c], outs[4].at[:, c], sem.at[4]).start()
        pltpu.make_async_copy(pvg.at[:, c], outs[5].at[:, c], sem.at[5]).start()
        return carry

    lax.fori_loop(0, heads // GROUP, some, 0)
    for j in range(4):
        pltpu.make_async_copy(ready[j], outs[j], sem.at[j]).wait()
    pltpu.make_async_copy(pkg, outs[4], sem.at[4]).wait()
    pltpu.make_async_copy(pvg, outs[5], sem.at[5]).wait()


def body(nh, ns, queries, keys, values, cotangent, prefix_keys, prefix_values, gain, lengths):
    rows, cols = queries.shape
    heads = cols // HEAD_DIM
    nown = heads // 2
    nb = rows // BLOCK
    any_spec = pl.BlockSpec(memory_space=pl.ANY)
    big = pltpu.VMEM((rows, cols), BF16)
    row = pltpu.VMEM((rows, HEAD_DIM), F32)
    units = nown // UNIT
    states = [pltpu.VMEM((units, SUB, UNIT * HEAD_DIM // SUB, HEAD_DIM), F32)] * 9
    scratch = (
        [big] * 5
        + [
            pltpu.VMEM((rows, cols), F32),
            pltpu.VMEM((heads, nb, BLOCK, BLOCK), BF16),
            pltpu.VMEM((1, UNIT, nb, BLOCK, BLOCK), BF16),
            pltpu.VMEM((heads, max(nb - 1, 1), HEAD_DIM, HEAD_DIM), F32),
            pltpu.VMEM((heads, nb, HEAD_DIM, HEAD_DIM), BF16),
            pltpu.VMEM((heads, max(nb - 1, 1), HEAD_DIM, HEAD_DIM), BF16),
            row,
            row,
            row,
            row,
        ]
        + [
            pltpu.VMEM((2 * rows // HEAD_DIM, HEAD_DIM), F32),
            pltpu.VMEM((max(nh - 1, 1), 2 * rows // HEAD_DIM, HEAD_DIM), F32),
        ]
        + states
        + states
        + [
            pltpu.SemaphoreType.DMA((13,)),
            pltpu.SemaphoreType.DMA((max(nh - 1, 1),)),
            pltpu.SemaphoreType.DMA((max(nh - 1, 1),)),
            pltpu.SemaphoreType.DMA((2, 4)),
            pltpu.SemaphoreType.DMA((2, 4, units * SUB)),
            pltpu.VMEM((1, cols), F32),
        ]
    )
    fast = pl.BlockSpec(memory_space=pltpu.VMEM)
    tot = pltpu.VMEM((heads, HEAD_DIM, HEAD_DIM), F32)
    wide = [queries, keys, values, cotangent, prefix_keys, prefix_values]
    wide.append(gain.reshape(1, cols))
    wide = [pltpu.with_memory_space_constraint(x, pltpu.HBM) for x in wide]
    made = pl.pallas_call(
        functools.partial(kernel, nh, ns, float(cols * nh)),
        out_shape=[big] * 6 + [tot],
        in_specs=[any_spec] * 7 + [pl.BlockSpec(memory_space=pltpu.SMEM)],
        out_specs=[fast] * 7,
        scratch_shapes=scratch,
        compiler_params=pltpu.CompilerParams(
            collective_id=0, has_side_effects=True, vmem_limit_bytes=38 * 1024 * 1024
        ),
    )(*wide, lengths)
    made = [pltpu.with_memory_space_constraint(x, pltpu.VMEM) for x in made]
    out = pltpu.HBM((rows, cols), BF16)
    return tuple(
        pl.pallas_call(
            finish,
            out_shape=[out] * 6,
            in_specs=[fast] * 7,
            out_specs=[any_spec] * 6,
            scratch_shapes=[big, big, pltpu.SemaphoreType.DMA((6,))],
            compiler_params=pltpu.CompilerParams(vmem_limit_bytes=8 * 1024 * 1024),
        )(*made)
    )


def solution(mesh):
    nh, ns = mesh.shape["head"], mesh.shape["seq"]
    tok = P("seq", "head")
    return jax.shard_map(
        functools.partial(body, nh, ns),
        mesh=mesh,
        in_specs=(tok,) * 6 + (P("head"), P("seq")),
        out_specs=(tok,) * 6,
        check_vma=False,
    )
```

```python
import functools

import jax
import jax.numpy as jnp
from jax import lax
from jax.experimental import pallas as pl
from jax.experimental.pallas import tpu as pltpu
from jax.sharding import PartitionSpec as P

HEAD_DIM = 128
BLOCK = 256
EPS = 1e-06
MESH = pl.DeviceIdType.MESH
F32 = jnp.float32
BF16 = jnp.bfloat16
UNIT = 2
SUB = 2
SKEW = 3
STAGES = 2
AHEAD = 2
GROUP = 4
PLAN = {
    4: (
        ([0, 3, 6, 9], [9, 6, 3, 0], [10, 7, 7, 10], [(4, 2, 1, 16, 99, 1, 1), (2, 1, 1, 16, 99, 1, 1), (2, 1, 1, 16, 99, 1, 1), (4, 2, 1, 16, 99, 1, 1)]),
        ([0, 3, 6, 9], [9, 6, 3, 0], [10, 7, 7, 10], [(4, 2, 1, 10, 9, 1, 1), (2, 1, 1, 16, 99, 1, 1), (2, 1, 1, 16, 99, 1, 1), (4, 2, 1, 10, 9, 1, 1)]),
    )
}


def mm(a, b, ca, cb):
    return lax.dot_general(a, b, (((ca,), (cb,)), ((), ())), preferred_element_type=F32)


def clip(value, top):
    if isinstance(value, int):
        return min(max(value, 0), top)
    return jnp.minimum(jnp.maximum(value, 0), top)


def done_by(s, row, total):
    first, up, down, count, second, up2, down2 = row
    fast = clip((s + 1 - first) * up // down, count)
    return fast + clip((s + 1 - second) * up2 // down2, total - count)


def timetable(nz, units, ph):
    pieces = units * SUB
    total = 2 * units * STAGES
    if nz in PLAN:
        right, left, other, work = PLAN[nz][ph]
    else:
        right = [SKEW * k for k in range(nz)]
        left = [SKEW * (nz - 1 - k) for k in range(nz)]
        other, work = [SKEW * (nz - 1) + SUB] * nz, [(2, 1, 1, total, 0, 1, 1)] * nz
    rows = []
    for k in range(nz):
        own = max(right[k], left[k])
        while any(
            done_by(u * SUB + own, work[k], total) < (u + 1) * STAGES
            for u in range(units)
        ):
            own += 1
        oth = max(other[k], own)
        while any(
            done_by(u * SUB + oth, work[k], total) < (units + u + 1) * STAGES
            for u in range(units)
        ):
            oth += 1
        last = pieces + oth
        while done_by(last - 1, work[k], total) < total:
            last += 1
        rows.append((right[k], left[k], own, oth, last) + tuple(work[k]))
    return rows


def kernel(nh, ns, width, *refs):
    (q_hbm, k_hbm, v_hbm, dy_hbm, pk_hbm, pv_hbm, gain_hbm, len_ref) = refs[:8]
    stage = refs[8:12]
    pk, pv, tout = refs[12:15]
    (q, k, v, dy, do, o, sc, ps, kv, mb, gb, sq, inn, rinv, coef) = refs[15:30]
    st_out, st_in = refs[30:32]
    bufs = (refs[32:41], refs[41:50])
    in_sem, st_recv, given, recv_sem, gain_ref = refs[50:55]

    rows, cols = q.shape
    heads = cols // HEAD_DIM
    nown = heads // 2
    units = nown // UNIT
    nb = rows // BLOCK
    nz = ns // 2
    me_h = lax.axis_index("head")
    me_s = lax.axis_index("seq")
    z = me_s // 2
    core = me_s % 2
    own0 = core * nown
    oth0 = (1 - core) * nown
    partner = (me_h, z * 2 + 1 - core)
    right = (me_h, jnp.minimum(me_s + 2, ns - 1))
    left = (me_h, jnp.maximum(me_s - 2, 0))
    not_first = z > 0
    not_last = z < nz - 1

    def cs(h):
        return pl.ds(pl.multiple_of(h * HEAD_DIM, HEAD_DIM), HEAD_DIM)

    def part(j, src, dst, head, count):
        c = pl.ds(pl.multiple_of(head * HEAD_DIM, HEAD_DIM), count * HEAD_DIM)
        return pltpu.make_async_copy(src.at[:, c], dst.at[:, c], in_sem.at[j])

    loads = [
        part(0, pk_hbm, pk, oth0, UNIT),
        part(1, pv_hbm, pv, oth0, UNIT),
        part(2, pk_hbm, pk, own0, UNIT),
        part(3, pv_hbm, pv, own0, UNIT),
        part(4, pk_hbm, pk, oth0 + UNIT, nown - UNIT),
        part(5, pv_hbm, pv, oth0 + UNIT, nown - UNIT),
        part(6, pk_hbm, pk, own0 + UNIT, nown - UNIT),
        part(7, pv_hbm, pv, own0 + UNIT, nown - UNIT),
        pltpu.make_async_copy(q_hbm, q, in_sem.at[8]),
        pltpu.make_async_copy(k_hbm, k, in_sem.at[9]),
        pltpu.make_async_copy(v_hbm, v, in_sem.at[10]),
        pltpu.make_async_copy(dy_hbm, dy, in_sem.at[11]),
        pltpu.make_async_copy(gain_hbm, gain_ref, in_sem.at[12]),
    ]
    for c in loads[:8]:
        c.start()

    barrier = pltpu.get_barrier_semaphore()
    pl.semaphore_signal(barrier, inc=1, device_id=partner, device_id_type=MESH)

    @pl.when(not_first)
    def _():
        pl.semaphore_signal(barrier, inc=1, device_id=left, device_id_type=MESH)

    @pl.when(not_last)
    def _():
        pl.semaphore_signal(barrier, inc=1, device_id=right, device_id_type=MESH)

    for d in range(1, nh):
        pl.semaphore_signal(
            barrier, inc=1, device_id=((me_h + d) % nh, me_s), device_id_type=MESH
        )

    sq[...] = jnp.zeros_like(sq)
    inn[...] = jnp.zeros_like(inn)
    for c in loads[:2]:
        c.wait()
    for c in loads[8:]:
        c.start()

    def causal():
        r = lax.broadcasted_iota(jnp.int32, (BLOCK, BLOCK), 0)
        c = lax.broadcasted_iota(jnp.int32, (BLOCK, BLOCK), 1)
        return r >= c

    def pick(values):
        found = jnp.int32(0)
        for k, value in enumerate(values):
            found = found + (z == k).astype(jnp.int32) * value
        return found

    plans = [timetable(nz, units, ph) for ph in range(2)]

    def exchange(ph, produce, compute, consume, ready, more):
        xo, xi, x, rin, rout, lin, lout, tot, tin = bufs[ph]
        pieces = units * SUB

        def hop(kind, src, dst, i, dev):
            return pltpu.make_async_remote_copy(
                src_ref=src,
                dst_ref=dst,
                send_sem=in_sem.at[kind],
                recv_sem=given.at[ph, i] if kind == 0 else recv_sem.at[ph, kind - 1, i],
                device_id=dev,
                device_id_type=MESH,
            )

        def to_partner(u):
            return hop(0, xo.at[u], xi.at[u], u, partner)

        def total_out(i):
            return hop(1, tot.at[i // SUB, i % SUB], tin.at[i // SUB, i % SUB], i, partner)

        def to_right(i):
            return hop(2, rout.at[i // SUB, i % SUB], rin.at[i // SUB, i % SUB], i, right)

        def to_left(i):
            return hop(3, lout.at[i // SUB, i % SUB], lin.at[i // SUB, i % SUB], i, left)

        def make(dst, u, first):
            for j, state in enumerate(produce(first + u * UNIT)):
                per = SUB // UNIT
                dst[u, j * per : (j + 1) * per] = state.reshape(per, -1, HEAD_DIM)

        def give(u):
            make(xo, u, oth0)
            to_partner(u).start()

        def state_of(ref, i):
            per = SUB // UNIT
            first = i % UNIT * per
            return ref[i // UNIT, pl.ds(first, per)].reshape(HEAD_DIM, HEAD_DIM)

        make(xo, 0, oth0)
        ready(-2)
        to_partner(0).start()
        ready(-1)
        plan = [pick([p[j] for p in plans[ph]]) for j in range(12)]
        r_at, l_at, t_at, o_at, slots = plan[:5]
        total = 2 * units * STAGES

        def slot(s, carry):
            u = s // SUB
            fresh = s % SUB == 0

            @pl.when(fresh & (u < units))
            def _():
                make(x, u, own0)
                to_partner(u).wait_recv()
                x[u] = x[u] + xi[u]

            i_r = s - r_at

            @pl.when((i_r >= 0) & (i_r < pieces))
            def _():
                i, j = i_r // SUB, i_r % SUB

                @pl.when(not_first)
                def _():
                    to_right(i_r).wait_recv()
                    rout[i, j] = rin[i, j] + x[i, j]

                @pl.when(jnp.logical_not(not_first))
                def _():
                    rout[i, j] = x[i, j]

                @pl.when(not_last)
                def _():
                    to_right(i_r).start()

            i_l = s - l_at

            @pl.when((i_l >= 0) & (i_l < pieces))
            def _():
                i, j = i_l // SUB, i_l % SUB

                @pl.when(not_last)
                def _():
                    to_left(i_l).wait_recv()
                    lout[i, j] = lin[i, j] + x[i, j]

                @pl.when(jnp.logical_not(not_last))
                def _():
                    lout[i, j] = x[i, j]

                @pl.when(not_first)
                def _():
                    to_left(i_l).start()

            more(s)

            @pl.when(s == 0)
            def _():
                for ahead in range(1, min(AHEAD, units)):
                    give(ahead)

            @pl.when(fresh & (u + AHEAD < units))
            def _():
                give(u + AHEAD)

            i_t = s - t_at

            @pl.when((i_t >= 0) & (i_t < pieces))
            def _():
                i, j = i_t // SUB, i_t % SUB

                @pl.when(not_last)
                def _():
                    tot[i, j] = rout[i, j] + lin[i, j]

                @pl.when(jnp.logical_not(not_last))
                def _():
                    tot[i, j] = rout[i, j]

                total_out(i_t).start()

            def chunk(w, carry):
                ready(w)
                h = (own0 + w // STAGES * UNIT) % heads
                for c in range(STAGES):

                    @pl.when(w % STAGES == c)
                    def _(c=c):
                        compute[c](h)

                return carry

            lax.fori_loop(done_by(s - 1, plan[5:], total), done_by(s, plan[5:], total), chunk, 0)

            per = SUB // UNIT

            @pl.when((i_t >= 0) & (i_t < pieces) & (i_t % per == per - 1))
            def _():
                consume(own0 + i_t // per, state_of(tot, i_t // per))

            i_o = s - o_at

            @pl.when((i_o >= 0) & (i_o < pieces) & (i_o % per == per - 1))
            def _():
                for j in range(per):
                    total_out(i_o // per * per + j).wait_recv()
                consume(oth0 + i_o // per, state_of(tin, i_o // per))

            return carry

        lax.fori_loop(0, slots, slot, 0)

        hop(0, xo, xi, 0, partner).wait_send()
        hop(1, tot, tin, 0, partner).wait_send()

        @pl.when(not_last)
        def _():
            hop(2, rout, rin, 0, right).wait_send()

        @pl.when(not_first)
        def _():
            hop(3, lout, lin, 0, left).wait_send()

    def blk(ref, c, h):
        return ref[pl.ds(c * BLOCK, BLOCK), cs(h)]

    def prefix_part(h):
        return [mm(pk[:, cs(h + j)], pv[:, cs(h + j)], 0, 0) for j in range(UNIT)]

    items = [(j, c) for j in range(UNIT) for c in range(nb)]

    def score(h):
        seen = causal()
        for j, c in items:
            a = mm(blk(q, c, h + j), blk(k, c, h + j), 1, 1)
            sc[h + j, c] = jnp.where(seen, a, 0.0).astype(BF16)

    def attend(h):
        for j, c in items:
            vc = blk(v, c, h + j)
            o[pl.ds(c * BLOCK, BLOCK), cs(h + j)] = mm(sc[h + j, c], vc, 1, 0)
            if c < nb - 1:
                add = mm(blk(k, c, h + j), vc, 0, 0)
                kv[h + j, c] = add if c == 0 else kv[h + j, c - 1] + add

    def loaded(s):
        if isinstance(s, int):
            if s == -2:
                pl.semaphore_wait(
                    barrier, nh + not_first.astype(jnp.int32) + not_last.astype(jnp.int32)
                )
            else:
                for c in loads[2:4]:
                    c.wait()
            return

        @pl.when(s == 0)
        def _():
            for c in loads[8:11]:
                c.wait()

        @pl.when(s == 1)
        def _():
            loads[11].wait()
            loads[12].wait()

    def loaded_rest(s):
        @pl.when(s == 0)
        def _():
            for c in loads[4:8]:
                c.wait()

    def use_state(h, state):
        g = gain_ref[:, cs(h)]
        for c in range(nb):
            r = pl.ds(c * BLOCK, BLOCK)
            st = (state if c == 0 else state + kv[h, c - 1]).astype(BF16)
            mb[h, c] = st
            oc = o[r, cs(h)] + mm(blk(q, c, h), st, 1, 0)
            o[r, cs(h)] = oc
            sq[r, :] += oc * oc
            inn[r, :] += blk(dy, c, h).astype(F32) * g * oc

    exchange(0, prefix_part, (score, attend), use_state, loaded, loaded_rest)

    row_sq = jnp.sum(sq[...].T, axis=0, keepdims=True)
    row_in = jnp.sum(inn[...].T, axis=0, keepdims=True)
    lanes = rows // HEAD_DIM

    def fold(row):
        return [row[:, i * HEAD_DIM : (i + 1) * HEAD_DIM] for i in range(lanes)]

    def unfold(tile, first):
        return jnp.concatenate([tile[first + i : first + i + 1] for i in range(lanes)], axis=1)

    st_out[...] = jnp.concatenate(fold(row_sq) + fold(row_in), axis=0)
    copies = []
    for d in range(1, nh):
        copies.append(
            pltpu.make_async_remote_copy(
                src_ref=st_out,
                dst_ref=st_in.at[d - 1],
                send_sem=in_sem.at[3 + d],
                recv_sem=st_recv.at[d - 1],
                device_id=((me_h + d) % nh, me_s),
                device_id_type=MESH,
            )
        )
        copies[-1].start()
    total = st_out[...]
    for d in range(1, nh):
        copies[d - 1].wait_recv()
        total = total + st_in[d - 1]
    inv = 1.0 / jnp.sqrt(unfold(total, 0) / width + EPS)
    cf = unfold(total, lanes) * (inv * inv * inv) / width
    live = lax.broadcasted_iota(jnp.int32, (1, rows), 1) < len_ref[0]
    inv = jnp.where(live, inv, 0.0)
    cf = jnp.where(live, cf, 0.0)
    rinv[...] = jnp.broadcast_to(inv, (HEAD_DIM, rows)).T
    coef[...] = jnp.broadcast_to(cf, (HEAD_DIM, rows)).T

    def state_grad(h):
        run = [None] * UNIT
        for c in reversed(range(nb)):
            r = pl.ds(c * BLOCK, BLOCK)
            ri, cf = rinv[r, :], coef[r, :]
            for j in range(UNIT):
                g = gain_ref[:, cs(h + j)]
                oc = o[r, cs(h + j)]
                stage[0][r, cs(h + j)] = (g * oc * ri).astype(BF16)
                d = (blk(dy, c, h + j).astype(F32) * g * ri - oc * cf).astype(BF16)
                do[r, cs(h + j)] = d
                if c < nb - 1:
                    gb[h + j, c] = run[j].astype(BF16)
                part = mm(blk(q, c, h + j), d, 0, 0)
                run[j] = part if run[j] is None else run[j] + part
        return run

    def query_side(h):
        seen = causal()
        for j, c in items:
            dc = blk(do, c, h + j)
            p = jnp.where(seen, mm(dc, blk(v, c, h + j), 1, 1), 0.0).astype(BF16)
            ps[0, j, c] = p
            qg = mm(dc, mb[h + j, c], 1, 1) + mm(p, blk(k, c, h + j), 1, 0)
            stage[1][pl.ds(c * BLOCK, BLOCK), cs(h + j)] = qg.astype(BF16)

    def key_side(h):
        for j, c in items:
            r = pl.ds(c * BLOCK, BLOCK)
            kg = mm(ps[0, j, c], blk(q, c, h + j), 0, 0)
            vg = mm(sc[h + j, c], blk(do, c, h + j), 0, 0)
            if c < nb - 1:
                g = gb[h + j, c]
                kg = kg + mm(blk(v, c, h + j), g, 1, 1)
                vg = vg + mm(blk(k, c, h + j), g, 1, 0)
            stage[2][r, cs(h + j)] = kg.astype(BF16)
            stage[3][r, cs(h + j)] = vg.astype(BF16)

    def keep_total(h, state):
        tout[h] = state

    exchange(1, state_grad, (query_side, key_side), keep_total, lambda s: None, lambda s: None)
    for c in copies:
        c.wait_send()


def finish(*refs):
    ready = refs[:4]
    pk, pv, total = refs[4:7]
    outs = refs[7:13]
    pkg, pvg, sem = refs[13:16]
    heads = total.shape[0]
    for j in range(4):
        pltpu.make_async_copy(ready[j], outs[j], sem.at[j]).start()

    def some(i, carry):
        for j in range(GROUP):
            h = i * GROUP + j
            c = pl.ds(pl.multiple_of(h * HEAD_DIM, HEAD_DIM), HEAD_DIM)
            state = total[h]
            hi = state.astype(BF16)
            lo = (state - hi.astype(F32)).astype(BF16)
            vals, keys = pv[:, c], pk[:, c]
            vv = jnp.concatenate([vals, vals], axis=1)
            kk = jnp.concatenate([keys, keys], axis=1)
            pkg[:, c] = mm(vv, jnp.concatenate([hi, lo], axis=1), 1, 1).astype(BF16)
            pvg[:, c] = mm(kk, jnp.concatenate([hi, lo], axis=0), 1, 0).astype(BF16)
        c = pl.ds(pl.multiple_of(i * GROUP * HEAD_DIM, HEAD_DIM), GROUP * HEAD_DIM)
        pltpu.make_async_copy(pkg.at[:, c], outs[4].at[:, c], sem.at[4]).start()
        pltpu.make_async_copy(pvg.at[:, c], outs[5].at[:, c], sem.at[5]).start()
        return carry

    lax.fori_loop(0, heads // GROUP, some, 0)
    for j in range(4):
        pltpu.make_async_copy(ready[j], outs[j], sem.at[j]).wait()
    pltpu.make_async_copy(pkg, outs[4], sem.at[4]).wait()
    pltpu.make_async_copy(pvg, outs[5], sem.at[5]).wait()


def body(nh, ns, queries, keys, values, cotangent, prefix_keys, prefix_values, gain, lengths):
    rows, cols = queries.shape
    heads = cols // HEAD_DIM
    nown = heads // 2
    nb = rows // BLOCK
    any_spec = pl.BlockSpec(memory_space=pl.ANY)
    big = pltpu.VMEM((rows, cols), BF16)
    row = pltpu.VMEM((rows, HEAD_DIM), F32)
    units = nown // UNIT
    states = [pltpu.VMEM((units, SUB, UNIT * HEAD_DIM // SUB, HEAD_DIM), F32)] * 9
    scratch = (
        [big] * 5
        + [
            pltpu.VMEM((rows, cols), F32),
            pltpu.VMEM((heads, nb, BLOCK, BLOCK), BF16),
            pltpu.VMEM((1, UNIT, nb, BLOCK, BLOCK), BF16),
            pltpu.VMEM((heads, max(nb - 1, 1), HEAD_DIM, HEAD_DIM), F32),
            pltpu.VMEM((heads, nb, HEAD_DIM, HEAD_DIM), BF16),
            pltpu.VMEM((heads, max(nb - 1, 1), HEAD_DIM, HEAD_DIM), BF16),
            row,
            row,
            row,
            row,
        ]
        + [
            pltpu.VMEM((2 * rows // HEAD_DIM, HEAD_DIM), F32),
            pltpu.VMEM((max(nh - 1, 1), 2 * rows // HEAD_DIM, HEAD_DIM), F32),
        ]
        + states
        + states
        + [
            pltpu.SemaphoreType.DMA((max(13, 3 + nh),)),
            pltpu.SemaphoreType.DMA((max(nh - 1, 1),)),
            pltpu.SemaphoreType.DMA((2, units)),
            pltpu.SemaphoreType.DMA((2, 3, units * SUB)),
            pltpu.VMEM((1, cols), F32),
        ]
    )
    fast = pl.BlockSpec(memory_space=pltpu.VMEM)
    tot = pltpu.VMEM((heads, HEAD_DIM, HEAD_DIM), F32)
    wide = [queries, keys, values, cotangent, prefix_keys, prefix_values]
    wide.append(gain.reshape(1, cols))
    wide = [pltpu.with_memory_space_constraint(x, pltpu.HBM) for x in wide]
    made = pl.pallas_call(
        functools.partial(kernel, nh, ns, float(cols * nh)),
        out_shape=[big] * 6 + [tot],
        in_specs=[any_spec] * 7 + [pl.BlockSpec(memory_space=pltpu.SMEM)],
        out_specs=[fast] * 7,
        scratch_shapes=scratch,
        compiler_params=pltpu.CompilerParams(
            collective_id=0, has_side_effects=True, vmem_limit_bytes=38 * 1024 * 1024
        ),
    )(*wide, lengths)
    made = [pltpu.with_memory_space_constraint(x, pltpu.VMEM) for x in made]
    out = pltpu.HBM((rows, cols), BF16)
    return tuple(
        pl.pallas_call(
            finish,
            out_shape=[out] * 6,
            in_specs=[fast] * 7,
            out_specs=[any_spec] * 6,
            scratch_shapes=[big, big, pltpu.SemaphoreType.DMA((6,))],
            compiler_params=pltpu.CompilerParams(vmem_limit_bytes=8 * 1024 * 1024),
        )(*made)
    )


def solution(mesh):
    nh, ns = mesh.shape["head"], mesh.shape["seq"]
    tok = P("seq", "head")
    return jax.shard_map(
        functools.partial(body, nh, ns),
        mesh=mesh,
        in_specs=(tok,) * 6 + (P("head"), P("seq")),
        out_specs=(tok,) * 6,
        check_vma=False,
    )
```

```python
import functools

import jax
import jax.numpy as jnp
from jax import lax
from jax.experimental import pallas as pl
from jax.experimental.pallas import tpu as pltpu
from jax.sharding import PartitionSpec as P

HEAD_DIM = 128
BLOCK = 256
EPS = 1e-06
MESH = pl.DeviceIdType.MESH
F32 = jnp.float32
BF16 = jnp.bfloat16
UNIT = 2
SUB = 2
SKEW = 3
STAGES = 2
AHEAD = 2
GROUP = 2
PLAN = {
    4: (
        ([0, 3, 6, 9], [9, 6, 3, 0], [10, 7, 7, 10], [(4, 2, 1, 16, 99, 1, 1), (2, 1, 1, 16, 99, 1, 1), (2, 1, 1, 16, 99, 1, 1), (4, 2, 1, 16, 99, 1, 1)]),
        ([0, 3, 6, 9], [9, 6, 3, 0], [10, 7, 7, 10], [(4, 2, 1, 10, 9, 1, 1), (2, 1, 1, 16, 99, 1, 1), (2, 1, 1, 16, 99, 1, 1), (4, 2, 1, 10, 9, 1, 1)]),
    )
}


def mm(a, b, ca, cb):
    return lax.dot_general(a, b, (((ca,), (cb,)), ((), ())), preferred_element_type=F32)


def clip(value, top):
    if isinstance(value, int):
        return min(max(value, 0), top)
    return jnp.minimum(jnp.maximum(value, 0), top)


def done_by(s, row, total):
    first, up, down, count, second, up2, down2 = row
    fast = clip((s + 1 - first) * up // down, count)
    return fast + clip((s + 1 - second) * up2 // down2, total - count)


def timetable(nz, units, ph):
    pieces = units * SUB
    total = 2 * units * STAGES
    if nz in PLAN:
        right, left, other, work = PLAN[nz][ph]
    else:
        right = [SKEW * k for k in range(nz)]
        left = [SKEW * (nz - 1 - k) for k in range(nz)]
        other, work = [SKEW * (nz - 1) + SUB] * nz, [(2, 1, 1, total, 0, 1, 1)] * nz
    rows = []
    for k in range(nz):
        own = max(right[k], left[k])
        while any(
            done_by(u * SUB + own, work[k], total) < (u + 1) * STAGES
            for u in range(units)
        ):
            own += 1
        oth = max(other[k], own)
        while any(
            done_by(u * SUB + oth, work[k], total) < (units + u + 1) * STAGES
            for u in range(units)
        ):
            oth += 1
        last = pieces + oth
        while done_by(last - 1, work[k], total) < total:
            last += 1
        rows.append((right[k], left[k], own, oth, last) + tuple(work[k]))
    return rows


def kernel(nh, ns, width, *refs):
    (q_hbm, k_hbm, v_hbm, dy_hbm, pk_hbm, pv_hbm, gain_hbm, len_ref) = refs[:8]
    stage = refs[8:12]
    pk, pv, tout = refs[12:15]
    (q, k, v, dy, do, o, sc, ps, kv, mb, gb, sq, inn, rinv, coef) = refs[15:30]
    st_out, st_in = refs[30:32]
    bufs = (refs[32:41], refs[41:50])
    in_sem, st_recv, given, recv_sem, gain_ref = refs[50:55]

    rows, cols = q.shape
    heads = cols // HEAD_DIM
    nown = heads // 2
    units = nown // UNIT
    nb = rows // BLOCK
    nz = ns // 2
    me_h = lax.axis_index("head")
    me_s = lax.axis_index("seq")
    z = me_s // 2
    core = me_s % 2
    own0 = core * nown
    oth0 = (1 - core) * nown
    partner = (me_h, z * 2 + 1 - core)
    right = (me_h, jnp.minimum(me_s + 2, ns - 1))
    left = (me_h, jnp.maximum(me_s - 2, 0))
    not_first = z > 0
    not_last = z < nz - 1

    def cs(h):
        return pl.ds(pl.multiple_of(h * HEAD_DIM, HEAD_DIM), HEAD_DIM)

    def part(j, src, dst, head, count):
        c = pl.ds(pl.multiple_of(head * HEAD_DIM, HEAD_DIM), count * HEAD_DIM)
        return pltpu.make_async_copy(src.at[:, c], dst.at[:, c], in_sem.at[j])

    loads = [
        part(0, pk_hbm, pk, oth0, UNIT),
        part(1, pv_hbm, pv, oth0, UNIT),
        part(2, pk_hbm, pk, own0, UNIT),
        part(3, pv_hbm, pv, own0, UNIT),
        part(4, pk_hbm, pk, oth0 + UNIT, nown - UNIT),
        part(5, pv_hbm, pv, oth0 + UNIT, nown - UNIT),
        part(6, pk_hbm, pk, own0 + UNIT, nown - UNIT),
        part(7, pv_hbm, pv, own0 + UNIT, nown - UNIT),
        pltpu.make_async_copy(q_hbm, q, in_sem.at[8]),
        pltpu.make_async_copy(k_hbm, k, in_sem.at[9]),
        pltpu.make_async_copy(v_hbm, v, in_sem.at[10]),
        pltpu.make_async_copy(dy_hbm, dy, in_sem.at[11]),
        pltpu.make_async_copy(gain_hbm, gain_ref, in_sem.at[12]),
    ]
    for c in loads[:8]:
        c.start()

    barrier = pltpu.get_barrier_semaphore()
    pl.semaphore_signal(barrier, inc=1, device_id=partner, device_id_type=MESH)

    @pl.when(not_first)
    def _():
        pl.semaphore_signal(barrier, inc=1, device_id=left, device_id_type=MESH)

    @pl.when(not_last)
    def _():
        pl.semaphore_signal(barrier, inc=1, device_id=right, device_id_type=MESH)

    for d in range(1, nh):
        pl.semaphore_signal(
            barrier, inc=1, device_id=((me_h + d) % nh, me_s), device_id_type=MESH
        )

    sq[...] = jnp.zeros_like(sq)
    inn[...] = jnp.zeros_like(inn)
    for c in loads[:2]:
        c.wait()
    for c in loads[8:]:
        c.start()

    def causal():
        r = lax.broadcasted_iota(jnp.int32, (BLOCK, BLOCK), 0)
        c = lax.broadcasted_iota(jnp.int32, (BLOCK, BLOCK), 1)
        return r >= c

    def pick(values):
        found = jnp.int32(0)
        for k, value in enumerate(values):
            found = found + (z == k).astype(jnp.int32) * value
        return found

    plans = [timetable(nz, units, ph) for ph in range(2)]

    def exchange(ph, produce, compute, consume, ready, more):
        xo, xi, x, rin, rout, lin, lout, tot, tin = bufs[ph]
        pieces = units * SUB

        def hop(kind, src, dst, i, dev):
            return pltpu.make_async_remote_copy(
                src_ref=src,
                dst_ref=dst,
                send_sem=in_sem.at[kind],
                recv_sem=given.at[ph, i] if kind == 0 else recv_sem.at[ph, kind - 1, i],
                device_id=dev,
                device_id_type=MESH,
            )

        def to_partner(u):
            return hop(0, xo.at[u], xi.at[u], u, partner)

        def total_out(i):
            return hop(1, tot.at[i // SUB, i % SUB], tin.at[i // SUB, i % SUB], i, partner)

        def to_right(i):
            return hop(2, rout.at[i // SUB, i % SUB], rin.at[i // SUB, i % SUB], i, right)

        def to_left(i):
            return hop(3, lout.at[i // SUB, i % SUB], lin.at[i // SUB, i % SUB], i, left)

        def make(dst, u, first):
            for j, state in enumerate(produce(first + u * UNIT)):
                per = SUB // UNIT
                dst[u, j * per : (j + 1) * per] = state.reshape(per, -1, HEAD_DIM)

        def give(u):
            make(xo, u, oth0)
            to_partner(u).start()

        def state_of(ref, i):
            per = SUB // UNIT
            first = i % UNIT * per
            return ref[i // UNIT, pl.ds(first, per)].reshape(HEAD_DIM, HEAD_DIM)

        make(xo, 0, oth0)
        ready(-2)
        to_partner(0).start()
        ready(-1)
        plan = [pick([p[j] for p in plans[ph]]) for j in range(12)]
        r_at, l_at, t_at, o_at, slots = plan[:5]
        total = 2 * units * STAGES

        def slot(s, carry):
            u = s // SUB
            fresh = s % SUB == 0

            @pl.when(fresh & (u < units))
            def _():
                make(x, u, own0)
                to_partner(u).wait_recv()
                x[u] = x[u] + xi[u]

            i_r = s - r_at

            @pl.when((i_r >= 0) & (i_r < pieces))
            def _():
                i, j = i_r // SUB, i_r % SUB

                @pl.when(not_first)
                def _():
                    to_right(i_r).wait_recv()
                    rout[i, j] = rin[i, j] + x[i, j]

                @pl.when(jnp.logical_not(not_first))
                def _():
                    rout[i, j] = x[i, j]

                @pl.when(not_last)
                def _():
                    to_right(i_r).start()

            i_l = s - l_at

            @pl.when((i_l >= 0) & (i_l < pieces))
            def _():
                i, j = i_l // SUB, i_l % SUB

                @pl.when(not_last)
                def _():
                    to_left(i_l).wait_recv()
                    lout[i, j] = lin[i, j] + x[i, j]

                @pl.when(jnp.logical_not(not_last))
                def _():
                    lout[i, j] = x[i, j]

                @pl.when(not_first)
                def _():
                    to_left(i_l).start()

            more(s)

            @pl.when(s == 0)
            def _():
                for ahead in range(1, min(AHEAD, units)):
                    give(ahead)

            @pl.when(fresh & (u + AHEAD < units))
            def _():
                give(u + AHEAD)

            i_t = s - t_at

            @pl.when((i_t >= 0) & (i_t < pieces))
            def _():
                i, j = i_t // SUB, i_t % SUB

                @pl.when(not_last)
                def _():
                    tot[i, j] = rout[i, j] + lin[i, j]

                @pl.when(jnp.logical_not(not_last))
                def _():
                    tot[i, j] = rout[i, j]

                total_out(i_t).start()

            def chunk(w, carry):
                ready(w)
                h = (own0 + w // STAGES * UNIT) % heads
                for c in range(STAGES):

                    @pl.when(w % STAGES == c)
                    def _(c=c):
                        compute[c](h)

                return carry

            lax.fori_loop(done_by(s - 1, plan[5:], total), done_by(s, plan[5:], total), chunk, 0)

            per = SUB // UNIT

            @pl.when((i_t >= 0) & (i_t < pieces) & (i_t % per == per - 1))
            def _():
                consume(own0 + i_t // per, state_of(tot, i_t // per))

            i_o = s - o_at

            @pl.when((i_o >= 0) & (i_o < pieces) & (i_o % per == per - 1))
            def _():
                for j in range(per):
                    total_out(i_o // per * per + j).wait_recv()
                consume(oth0 + i_o // per, state_of(tin, i_o // per))

            return carry

        lax.fori_loop(0, slots, slot, 0)

        hop(0, xo, xi, 0, partner).wait_send()
        hop(1, tot, tin, 0, partner).wait_send()

        @pl.when(not_last)
        def _():
            hop(2, rout, rin, 0, right).wait_send()

        @pl.when(not_first)
        def _():
            hop(3, lout, lin, 0, left).wait_send()

    def blk(ref, c, h):
        return ref[pl.ds(c * BLOCK, BLOCK), cs(h)]

    def prefix_part(h):
        return [mm(pk[:, cs(h + j)], pv[:, cs(h + j)], 0, 0) for j in range(UNIT)]

    items = [(j, c) for j in range(UNIT) for c in range(nb)]

    def score(h):
        seen = causal()
        for j, c in items:
            a = mm(blk(q, c, h + j), blk(k, c, h + j), 1, 1)
            sc[h + j, c] = jnp.where(seen, a, 0.0).astype(BF16)

    def attend(h):
        for j, c in items:
            vc = blk(v, c, h + j)
            o[pl.ds(c * BLOCK, BLOCK), cs(h + j)] = mm(sc[h + j, c], vc, 1, 0)
            if c < nb - 1:
                add = mm(blk(k, c, h + j), vc, 0, 0)
                kv[h + j, c] = add if c == 0 else kv[h + j, c - 1] + add

    def loaded(s):
        if isinstance(s, int):
            if s == -2:
                pl.semaphore_wait(
                    barrier, nh + not_first.astype(jnp.int32) + not_last.astype(jnp.int32)
                )
            else:
                for c in loads[2:4]:
                    c.wait()
            return

        @pl.when(s == 0)
        def _():
            for c in loads[8:11]:
                c.wait()

        @pl.when(s == 1)
        def _():
            loads[11].wait()
            loads[12].wait()

    def loaded_rest(s):
        @pl.when(s == 0)
        def _():
            for c in loads[4:8]:
                c.wait()

    def use_state(h, state):
        g = gain_ref[:, cs(h)]
        for c in range(nb):
            r = pl.ds(c * BLOCK, BLOCK)
            st = (state if c == 0 else state + kv[h, c - 1]).astype(BF16)
            mb[h, c] = st
            oc = o[r, cs(h)] + mm(blk(q, c, h), st, 1, 0)
            o[r, cs(h)] = oc
            sq[r, :] += oc * oc
            inn[r, :] += blk(dy, c, h).astype(F32) * g * oc

    exchange(0, prefix_part, (score, attend), use_state, loaded, loaded_rest)

    row_sq = jnp.sum(sq[...].T, axis=0, keepdims=True)
    row_in = jnp.sum(inn[...].T, axis=0, keepdims=True)
    lanes = rows // HEAD_DIM

    def fold(row):
        return [row[:, i * HEAD_DIM : (i + 1) * HEAD_DIM] for i in range(lanes)]

    def unfold(tile, first):
        return jnp.concatenate([tile[first + i : first + i + 1] for i in range(lanes)], axis=1)

    st_out[...] = jnp.concatenate(fold(row_sq) + fold(row_in), axis=0)
    copies = []
    for d in range(1, nh):
        copies.append(
            pltpu.make_async_remote_copy(
                src_ref=st_out,
                dst_ref=st_in.at[d - 1],
                send_sem=in_sem.at[3 + d],
                recv_sem=st_recv.at[d - 1],
                device_id=((me_h + d) % nh, me_s),
                device_id_type=MESH,
            )
        )
        copies[-1].start()
    total = st_out[...]
    for d in range(1, nh):
        copies[d - 1].wait_recv()
        total = total + st_in[d - 1]
    inv = 1.0 / jnp.sqrt(unfold(total, 0) / width + EPS)
    cf = unfold(total, lanes) * (inv * inv * inv) / width
    live = lax.broadcasted_iota(jnp.int32, (1, rows), 1) < len_ref[0]
    inv = jnp.where(live, inv, 0.0)
    cf = jnp.where(live, cf, 0.0)
    rinv[...] = jnp.broadcast_to(inv, (HEAD_DIM, rows)).T
    coef[...] = jnp.broadcast_to(cf, (HEAD_DIM, rows)).T

    def state_grad(h):
        run = [None] * UNIT
        for c in reversed(range(nb)):
            r = pl.ds(c * BLOCK, BLOCK)
            ri, cf = rinv[r, :], coef[r, :]
            for j in range(UNIT):
                g = gain_ref[:, cs(h + j)]
                oc = o[r, cs(h + j)]
                stage[0][r, cs(h + j)] = (g * oc * ri).astype(BF16)
                d = (blk(dy, c, h + j).astype(F32) * g * ri - oc * cf).astype(BF16)
                do[r, cs(h + j)] = d
                if c < nb - 1:
                    gb[h + j, c] = run[j].astype(BF16)
                part = mm(blk(q, c, h + j), d, 0, 0)
                run[j] = part if run[j] is None else run[j] + part
        return run

    def query_side(h):
        seen = causal()
        for j, c in items:
            dc = blk(do, c, h + j)
            p = jnp.where(seen, mm(dc, blk(v, c, h + j), 1, 1), 0.0).astype(BF16)
            ps[0, j, c] = p
            qg = mm(dc, mb[h + j, c], 1, 1) + mm(p, blk(k, c, h + j), 1, 0)
            stage[1][pl.ds(c * BLOCK, BLOCK), cs(h + j)] = qg.astype(BF16)

    def key_side(h):
        for j, c in items:
            r = pl.ds(c * BLOCK, BLOCK)
            kg = mm(ps[0, j, c], blk(q, c, h + j), 0, 0)
            vg = mm(sc[h + j, c], blk(do, c, h + j), 0, 0)
            if c < nb - 1:
                g = gb[h + j, c]
                kg = kg + mm(blk(v, c, h + j), g, 1, 1)
                vg = vg + mm(blk(k, c, h + j), g, 1, 0)
            stage[2][r, cs(h + j)] = kg.astype(BF16)
            stage[3][r, cs(h + j)] = vg.astype(BF16)

    def keep_total(h, state):
        tout[h] = state

    exchange(1, state_grad, (query_side, key_side), keep_total, lambda s: None, lambda s: None)
    for c in copies:
        c.wait_send()


def finish(*refs):
    ready = refs[:4]
    pk, pv, total = refs[4:7]
    outs = refs[7:13]
    pkg, pvg, sem = refs[13:16]
    heads = total.shape[0]
    for j in range(4):
        pltpu.make_async_copy(ready[j], outs[j], sem.at[j]).start()

    def some(i, carry):
        for j in range(GROUP):
            h = i * GROUP + j
            c = pl.ds(pl.multiple_of(h * HEAD_DIM, HEAD_DIM), HEAD_DIM)
            state = total[h]
            hi = state.astype(BF16)
            lo = (state - hi.astype(F32)).astype(BF16)
            vals, keys = pv[:, c], pk[:, c]
            vv = jnp.concatenate([vals, vals], axis=1)
            kk = jnp.concatenate([keys, keys], axis=1)
            pkg[:, c] = mm(vv, jnp.concatenate([hi, lo], axis=1), 1, 1).astype(BF16)
            pvg[:, c] = mm(kk, jnp.concatenate([hi, lo], axis=0), 1, 0).astype(BF16)
        c = pl.ds(pl.multiple_of(i * GROUP * HEAD_DIM, HEAD_DIM), GROUP * HEAD_DIM)
        pltpu.make_async_copy(pkg.at[:, c], outs[4].at[:, c], sem.at[4]).start()
        pltpu.make_async_copy(pvg.at[:, c], outs[5].at[:, c], sem.at[5]).start()
        return carry

    lax.fori_loop(0, heads // GROUP, some, 0)
    for j in range(4):
        pltpu.make_async_copy(ready[j], outs[j], sem.at[j]).wait()
    pltpu.make_async_copy(pkg, outs[4], sem.at[4]).wait()
    pltpu.make_async_copy(pvg, outs[5], sem.at[5]).wait()


def body(nh, ns, queries, keys, values, cotangent, prefix_keys, prefix_values, gain, lengths):
    rows, cols = queries.shape
    heads = cols // HEAD_DIM
    nown = heads // 2
    nb = rows // BLOCK
    any_spec = pl.BlockSpec(memory_space=pl.ANY)
    big = pltpu.VMEM((rows, cols), BF16)
    row = pltpu.VMEM((rows, HEAD_DIM), F32)
    units = nown // UNIT
    states = [pltpu.VMEM((units, SUB, UNIT * HEAD_DIM // SUB, HEAD_DIM), F32)] * 9
    scratch = (
        [big] * 5
        + [
            pltpu.VMEM((rows, cols), F32),
            pltpu.VMEM((heads, nb, BLOCK, BLOCK), BF16),
            pltpu.VMEM((1, UNIT, nb, BLOCK, BLOCK), BF16),
            pltpu.VMEM((heads, max(nb - 1, 1), HEAD_DIM, HEAD_DIM), F32),
            pltpu.VMEM((heads, nb, HEAD_DIM, HEAD_DIM), BF16),
            pltpu.VMEM((heads, max(nb - 1, 1), HEAD_DIM, HEAD_DIM), BF16),
            row,
            row,
            row,
            row,
        ]
        + [
            pltpu.VMEM((2 * rows // HEAD_DIM, HEAD_DIM), F32),
            pltpu.VMEM((max(nh - 1, 1), 2 * rows // HEAD_DIM, HEAD_DIM), F32),
        ]
        + states
        + states
        + [
            pltpu.SemaphoreType.DMA((max(13, 3 + nh),)),
            pltpu.SemaphoreType.DMA((max(nh - 1, 1),)),
            pltpu.SemaphoreType.DMA((2, units)),
            pltpu.SemaphoreType.DMA((2, 3, units * SUB)),
            pltpu.VMEM((1, cols), F32),
        ]
    )
    fast = pl.BlockSpec(memory_space=pltpu.VMEM)
    tot = pltpu.VMEM((heads, HEAD_DIM, HEAD_DIM), F32)
    wide = [queries, keys, values, cotangent, prefix_keys, prefix_values]
    wide.append(gain.reshape(1, cols))
    wide = [pltpu.with_memory_space_constraint(x, pltpu.HBM) for x in wide]
    made = pl.pallas_call(
        functools.partial(kernel, nh, ns, float(cols * nh)),
        out_shape=[big] * 6 + [tot],
        in_specs=[any_spec] * 7 + [pl.BlockSpec(memory_space=pltpu.SMEM)],
        out_specs=[fast] * 7,
        scratch_shapes=scratch,
        compiler_params=pltpu.CompilerParams(
            collective_id=0, has_side_effects=True, vmem_limit_bytes=38 * 1024 * 1024
        ),
    )(*wide, lengths)
    made = [pltpu.with_memory_space_constraint(x, pltpu.VMEM) for x in made]
    out = pltpu.HBM((rows, cols), BF16)
    return tuple(
        pl.pallas_call(
            finish,
            out_shape=[out] * 6,
            in_specs=[fast] * 7,
            out_specs=[any_spec] * 6,
            scratch_shapes=[big, big, pltpu.SemaphoreType.DMA((6,))],
            compiler_params=pltpu.CompilerParams(vmem_limit_bytes=8 * 1024 * 1024),
        )(*made)
    )


def solution(mesh):
    nh, ns = mesh.shape["head"], mesh.shape["seq"]
    tok = P("seq", "head")
    return jax.shard_map(
        functools.partial(body, nh, ns),
        mesh=mesh,
        in_specs=(tok,) * 6 + (P("head"), P("seq")),
        out_specs=(tok,) * 6,
        check_vma=False,
    )
```
